256 devices in a mesh: group: 8 (over x, z_lo), replica: 32 (over y, z_hi, core).
Axes of the slice: x: 4, y: 4, z: 8 (z_hi: 4, z_lo: 2; z = z_hi * 2 + z_lo), core: 2. Of those that a mesh axis runs over, the one named last changes fastest.
Arguments:
- hidden_in: bfloat16 [81920, 3072], P(('group', 'replica')), may hold values from -24 to 24
- w_query: bfloat16 [3072, 1536], replicated, may hold values from -0.109375 to 0.109375
- query_gain: float32 [128], replicated, may hold values from 0.5 to 2
- down_projection_matrix: bfloat16 [3072, 64], replicated, may hold values from -0.23925781 to 0.23925781
- up_projection_matrix: bfloat16 [64, 1536], replicated, may hold values from -0.59765625 to 0.59765625
- query_cotangent: bfloat16 [81920, 1536], P(('group', 'replica')), may hold values from -24 to 24
- first_moment: float32 [4608, 64], P(('group', 'replica')), may hold values from -3 to 3
- second_moment: float32 [4608, 64], P(('group', 'replica')), may hold values from 0.001 to 0.1
Outputs:
- new_down: bfloat16 [3072, 64], replicated
- new_up: bfloat16 [64, 1536], replicated
- first_next: float32 [4608, 64], P(('group', 'replica'))
- second_next: float32 [4608, 64], P(('group', 'replica'))
The draws below stay inside these ranges and needn't reach their ends.
All inputs are finite; a program needn't handle non-finite values.
Results may differ from the reference program's by a relative error of at most 0.0019.
Values may be sent and summed in bfloat16 or wider, within the bound.
A program may use at most 64 MiB of HBM per device.

```python
import math
import jax
import jax.numpy as jnp
from jax import lax

D = 3072
HD = 128
QW = 1536
R = 64
TOK_DEV = 320
TOKENS = 81920
ROWS = 4608
N_GROUP = 8
N_REPLICA = 32


def raised(array, key, source, target, shards_of, factor):
    def block_of(dim):
        return (jnp.arange(array.shape[dim]) // (array.shape[dim] // shards_of)).reshape((-1,) + (1,) * (array.ndim - 1 - dim))

    one_side = jax.random.permutation(key, shards_of)[block_of(target)]
    second = (block_of(target) + shards_of // 2) % shards_of
    return jnp.where((block_of(source) == one_side) | (block_of(source) == second), factor * array, array)


def block_levels(rng, extent, pieces, low, largest):
    loudness, own = 1.0, jax.random.fold_in(rng, 6)
    for dim, blocks in pieces:
        steps = jnp.exp(jax.random.uniform(jax.random.fold_in(own, dim), (blocks,), jnp.float32, low / len(pieces), largest / len(pieces)))
        loudness = loudness * jnp.repeat(steps, extent[dim] // blocks).reshape([-1 if axis == dim else 1 for axis in range(len(extent))])
    return loudness


def centred(stream_key, dims, width, reach, pieces=(), kind=jnp.bfloat16):
    loudness = block_levels(stream_key, dims, pieces, -0.22, 0.18) if pieces else 1.0
    array = jax.random.normal(stream_key, dims, jnp.float32) * width * loudness
    return jnp.minimum(jnp.maximum(array, -reach), reach).astype(kind)


def gaussian_with(key, extent, scale, bound, shards, heavy, held_as=jnp.bfloat16):
    values = scale * jax.random.normal(key, extent, jnp.float32)
    if shards:
        values = values * block_levels(key, extent, shards, -0.22, 0.18)
    return jnp.clip(raised(values, jax.random.fold_in(key, 3), *heavy), -bound, bound).astype(held_as)


def setup_inputs(seed: int = 0) -> dict:
    streams_of = jax.random.split(jax.random.key(seed), 9)
    return {
        "hidden_in": gaussian_with(streams_of[0], (TOKENS, D), 1.0, 24.0, ((0, 256),), (0, 1, 256, 6.0)),
        "w_query": centred(streams_of[1], (D, QW), D ** -0.5, 0.109375),
        "query_gain": jnp.clip(jnp.exp(jax.random.uniform(streams_of[2], (HD,), jnp.float32, math.log(0.5), math.log(2.0))), 0.5, 2.0),
        "down_projection_matrix": centred(streams_of[3], (D, R), 0.04, 0.23925781),
        "up_projection_matrix": centred(streams_of[4], (R, QW), 0.1, 0.59765625),
        "query_cotangent": gaussian_with(streams_of[5], (TOKENS, QW), 1.0, 24.0, ((0, 256),), (0, 1, 256, 6.0)),
        "first_moment": centred(streams_of[6], (ROWS, R), 0.5, 3.0, ((0, 256),), jnp.float32),
        "second_moment": jnp.clip(jnp.exp(math.log(0.1) - 4.6051702 * jax.random.uniform(streams_of[7], (ROWS, R), jnp.float32) ** block_levels(streams_of[7], (ROWS, R), ((0, 256),), -0.2, 0.2)), 0.001, 0.1),
    }


adapter_scale_factor = 0.5
norm_epsilon = 1e-06
beta_one = 0.9
beta_two = 0.999
first_bias = 1.0 - 0.9 ** 10
second_bias = 1.0 - 0.999 ** 10
learn_rate = 0.001
adam_eps = 1e-08

def queries_backward(rows_in, grads_in, w_query, query_gain, down_projection_matrix, up_projection_matrix):
    reduced_rank_input = jnp.dot(rows_in, down_projection_matrix, preferred_element_type=jnp.float32).astype(jnp.bfloat16)
    apply_projection = jnp.dot(rows_in, w_query, preferred_element_type=jnp.float32)
    apply_projection = apply_projection + adapter_scale_factor * jnp.dot(reduced_rank_input, up_projection_matrix, preferred_element_type=jnp.float32)
    token_count = apply_projection.shape[0]
    head_size = query_gain.shape[0]
    shaped = apply_projection.reshape(token_count, -1, head_size)
    inverse = lax.rsqrt(lax.optimization_barrier(jnp.mean(shaped * shaped, axis=-1, keepdims=True)) + norm_epsilon)
    normed = shaped * inverse
    upstream = grads_in.astype(jnp.float32).reshape(shaped.shape) * query_gain
    grad_pre = inverse * (upstream - normed * lax.optimization_barrier(jnp.mean(upstream * normed, axis=-1, keepdims=True)))
    grad_pre = grad_pre.reshape(token_count, -1).astype(jnp.bfloat16)
    backward_reduced = lax.dot_general(grad_pre, up_projection_matrix, (((1,), (1,)), ((), ())), preferred_element_type=jnp.float32)
    backward_reduced = (adapter_scale_factor * backward_reduced).astype(jnp.bfloat16)
    scaled_reduced = (reduced_rank_input.astype(jnp.float32) * adapter_scale_factor).astype(jnp.bfloat16)
    return (grad_pre, backward_reduced, scaled_reduced)

def adam_update(grads, params, first, second):
    first_new = beta_one * first + (1.0 - beta_one) * grads
    second_new = beta_two * second + (1.0 - beta_two) * grads * grads
    direction = first_new / first_bias / (jnp.sqrt(second_new / second_bias) + adam_eps)
    return ((params - learn_rate * direction).astype(jnp.bfloat16), first_new, second_new)

def reference(hidden_in, w_query, query_gain, down_projection_matrix, up_projection_matrix, query_cotangent, first_moment, second_moment):
    accelerator_list = N_GROUP * N_REPLICA
    rows_in = hidden_in.reshape(accelerator_list, TOK_DEV, D)
    grads_in = query_cotangent.reshape(accelerator_list, TOK_DEV, QW)

    def one_device(summed, inputs_pair):
        grad_pre, backward_reduced, scaled_reduced = queries_backward(inputs_pair[0], inputs_pair[1], w_query, query_gain, down_projection_matrix, up_projection_matrix)
        down_term = lax.dot_general(inputs_pair[0], backward_reduced, (((0,), (0,)), ((), ())), preferred_element_type=jnp.float32)
        up_term = lax.dot_general(grad_pre, scaled_reduced, (((0,), (0,)), ((), ())), preferred_element_type=jnp.float32)
        return (summed + jnp.concatenate([down_term, up_term], axis=0) / accelerator_list, None)
    grads, _ = lax.scan(one_device, jnp.zeros((D + QW, R), jnp.float32), (rows_in, grads_in))
    params = jnp.concatenate([down_projection_matrix, up_projection_matrix.T], axis=0).astype(jnp.float32)
    updated, first_new, second_new = adam_update(grads, params, first_moment, second_moment)
    return (updated[:D], updated[D:].T, first_new, second_new)
```

```python
import functools

import jax
import jax.numpy as jnp
from jax import lax
from jax.experimental import pallas as pl
from jax.experimental.pallas import tpu as pltpu
from jax.sharding import PartitionSpec as P

adapter_scale_factor = 0.5
norm_epsilon = 1e-06
beta_one = 0.9
beta_two = 0.999
first_bias = 1.0 - 0.9**10
second_bias = 1.0 - 0.999**10
learn_rate = 0.001
adam_eps = 1e-08

MESH = pl.DeviceIdType.MESH
NX, NY, NZH = 4, 4, 4
OWN = 18
HALF = 72
N_DEV = 256


def queries_backward(
    rows_in, grads_in, w_query, query_gain, down_projection_matrix, up_projection_matrix
):
    reduced_rank_input = jnp.dot(
        rows_in, down_projection_matrix, preferred_element_type=jnp.float32
    ).astype(jnp.bfloat16)
    apply_projection = jnp.dot(rows_in, w_query, preferred_element_type=jnp.float32)
    apply_projection = apply_projection + adapter_scale_factor * jnp.dot(
        reduced_rank_input, up_projection_matrix, preferred_element_type=jnp.float32
    )
    token_count = apply_projection.shape[0]
    head_size = query_gain.shape[0]
    shaped = apply_projection.reshape(token_count, -1, head_size)
    inverse = lax.rsqrt(jnp.mean(shaped * shaped, axis=-1, keepdims=True) + norm_epsilon)
    normed = shaped * inverse
    upstream = grads_in.astype(jnp.float32).reshape(shaped.shape) * query_gain
    grad_pre = inverse * (upstream - normed * jnp.mean(upstream * normed, axis=-1, keepdims=True))
    grad_pre = grad_pre.reshape(token_count, -1).astype(jnp.bfloat16)
    backward_reduced = lax.dot_general(
        grad_pre, up_projection_matrix, (((1,), (1,)), ((), ())), preferred_element_type=jnp.float32
    )
    backward_reduced = (adapter_scale_factor * backward_reduced).astype(jnp.bfloat16)
    scaled_reduced = (reduced_rank_input.astype(jnp.float32) * adapter_scale_factor).astype(
        jnp.bfloat16
    )
    return (grad_pre, backward_reduced, scaled_reduced)


def adam_update(grads, params, first, second):
    first_new = beta_one * first + (1.0 - beta_one) * grads
    second_new = beta_two * second + (1.0 - beta_two) * grads * grads
    direction = first_new / first_bias / (jnp.sqrt(second_new / second_bias) + adam_eps)
    return ((params - learn_rate * direction).astype(jnp.bfloat16), first_new, second_new)


def exchange_kernel(
    p_ref, par_ref, m_ref, v_ref,
    first_ref, second_ref, g_ref,
    cbuf, qf, qb, xbuf, zsend, zbuf, ubuf, abuf, rows, gbuf,
    cs, cr, xs, xr, zs, zr, us, ur, bs, br, fs, fr,
):
    g = lax.axis_index("group")
    r = lax.axis_index("replica")
    x, zl = g // 2, g % 2
    y, zh, c = r // 8, (r // 2) % 4, r % 2
    t_me = x * NY + y

    def dev(x_, y_, zh_, zl_, c_):
        return (x_ * 2 + zl_, y_ * 8 + zh_ * 2 + c_)

    def rdma(src, dst, ssem, rsem, to):
        return pltpu.make_async_remote_copy(
            src_ref=src, dst_ref=dst, send_sem=ssem, recv_sem=rsem,
            device_id=to, device_id_type=MESH)

    partner = dev(x, y, zh, zl, 1 - c)

    barrier = pltpu.get_barrier_semaphore()
    for d in range(1, 16):
        pl.semaphore_signal(
            barrier, inc=1, device_id_type=MESH,
            device_id=dev((x + d // 4) % NX, (y + d % 4) % NY, zh, zl, c))
    for d in range(1, 16):
        k = (zh * 4 + zl * 2 + c + d) % 16
        pl.semaphore_signal(
            barrier, inc=1, device_id_type=MESH,
            device_id=dev(x, y, k // 4, (k // 2) % 2, k % 2))
    pl.semaphore_wait(barrier, 30)

    to_partner = rdma(p_ref.at[1 - c], cbuf, cs, cr, partner)
    to_partner.start()
    to_partner.wait()
    q = p_ref[c] + cbuf[...]
    qb[...] = q.astype(jnp.bfloat16)
    qf[...] = p_ref[c, t_me] + cbuf[t_me]

    order = sorted(range(1, 16), key=lambda d: -(min(d // 4, 4 - d // 4) + min(d % 4, 4 - d % 4)))
    sends = []
    for d in order:
        tx, ty = (x + d // 4) % NX, (y + d % 4) % NY
        cp = rdma(qb.at[tx * NY + ty], xbuf.at[d], xs.at[d], xr.at[d], dev(tx, ty, zh, zl, c))
        cp.start()
        sends.append(cp)
    total = qf[...]
    for d, cp in zip(order, sends):
        cp.wait_recv()
        total = total + xbuf[d].astype(jnp.float32)
    for k in range(4):
        zsend[k] = total[OWN * k : OWN * (k + 1)]
    for cp in sends:
        cp.wait_send()

    own_z = zl == c
    zcopies = []
    for dh in range(4):
        for c2 in range(2):
            th = (zh + dh) % NZH
            slab = (th % 2) * 2 + c2
            slot = dh * 2 + zl
            j = dh * 2 + c2
            cp = rdma(zsend.at[slab], zbuf.at[slot], zs.at[j], zr.at[slot], dev(x, y, th, c, c2))
            if dh == 0:
                here = own_z & (c == c2)

                @pl.when(here)
                def _():
                    zbuf[slot] = zsend[slab]

                @pl.when(jnp.logical_not(here))
                def _():
                    cp.start()
            else:
                here = None
                cp.start()
            zcopies.append((cp, here))
    for slot in range(8):
        cp = rdma(zsend.at[0], zbuf.at[slot], zs.at[0], zr.at[slot], partner)
        if slot < 2:
            @pl.when(jnp.logical_not(own_z & (zl == slot)))
            def _():
                cp.wait_recv()
        else:
            cp.wait_recv()
    acc = zbuf[0]
    for slot in range(1, 8):
        acc = acc + zbuf[slot]
    for cp, here in zcopies:
        if here is None:
            cp.wait_send()
        else:
            @pl.when(jnp.logical_not(here))
            def _():
                cp.wait_send()
    grad = jnp.where(zh >= 2, acc[:, 64:], acc[:, :64]) / N_DEV

    updated, first_new, second_new = adam_update(grad, par_ref[...], m_ref[...], v_ref[...])
    first_ref[...] = first_new
    second_ref[...] = second_new
    ubuf[...] = updated

    k_me = zh * 2 + c
    ucopies = []
    for dh in range(4):
        for l2 in range(2):
            th = (zh + dh) % NZH
            j = dh * 2 + l2
            cp = rdma(ubuf, abuf.at[k_me], us.at[j], ur.at[k_me], dev(x, y, th, l2, zl))
            if dh == 0:
                here = own_z & (zl == l2)

                @pl.when(here)
                def _():
                    abuf[k_me] = ubuf[...]

                @pl.when(jnp.logical_not(here))
                def _():
                    cp.start()
            else:
                here = None
                cp.start()
            ucopies.append((cp, here))
    for k in range(8):
        cp = rdma(ubuf, abuf.at[k], us.at[0], ur.at[k], partner)

        @pl.when(jnp.logical_not(own_z & (k_me == k)))
        def _():
            cp.wait_recv()

        rows[OWN * k : OWN * (k + 1), :] = abuf[k].astype(jnp.float32)
    for cp, here in ucopies:
        if here is None:
            cp.wait_send()
        else:
            @pl.when(jnp.logical_not(here))
            def _():
                cp.wait_send()
    gbuf[c, t_me] = jnp.concatenate([rows[:HALF], rows[HALF:]], axis=1).astype(jnp.bfloat16)

    sends = []
    for d in order:
        tx, ty = (x + d // 4) % NX, (y + d % 4) % NY
        cp = rdma(gbuf.at[c, t_me], gbuf.at[c, t_me], bs.at[d], br.at[d], dev(tx, ty, zh, zl, c))
        cp.start()
        sends.append(cp)
    forwards = []
    cp = rdma(gbuf.at[c, t_me], gbuf.at[c, t_me], fs.at[0], fr.at[0], partner)
    cp.start()
    forwards.append(cp)
    for d in sorted(order, key=lambda d: (min(d // 4, 4 - d // 4) + min(d % 4, 4 - d % 4))):
        src = ((x + NX - d // 4) % NX) * NY + (y + NY - d % 4) % NY
        arrived = rdma(gbuf.at[c, src], gbuf.at[c, src], bs.at[d], br.at[d], partner)
        arrived.wait_recv()
        cp = rdma(gbuf.at[c, src], gbuf.at[c, src], fs.at[d], fr.at[d], partner)
        cp.start()
        forwards.append(cp)
    for cp in sends:
        cp.wait_send()
    for cp in forwards:
        cp.wait_send()
    for d in range(16):
        src = ((x + NX - d // 4) % NX) * NY + (y + NY - d % 4) % NY
        rdma(gbuf.at[1 - c, src], gbuf.at[1 - c, src], fs.at[d], fr.at[d], partner).wait_recv()
    g_ref[...] = gbuf[...]


def exchange(packed, params, first, second):
    vm = pl.BlockSpec(memory_space=pltpu.VMEM)
    dma = pltpu.SemaphoreType.DMA
    return pl.pallas_call(
        exchange_kernel,
        out_shape=(
            jax.ShapeDtypeStruct(first.shape, jnp.float32),
            jax.ShapeDtypeStruct(second.shape, jnp.float32),
            jax.ShapeDtypeStruct((2, 16, HALF, 128), jnp.bfloat16),
        ),
        in_specs=[vm] * 4,
        out_specs=(vm,) * 3,
        scratch_shapes=[
            pltpu.VMEM((16, HALF, 128), jnp.float32),
            pltpu.VMEM((HALF, 128), jnp.float32),
            pltpu.VMEM((16, HALF, 128), jnp.bfloat16),
            pltpu.VMEM((16, HALF, 128), jnp.bfloat16),
            pltpu.VMEM((4, OWN, 128), jnp.float32),
            pltpu.VMEM((8, OWN, 128), jnp.float32),
            pltpu.VMEM((OWN, 64), jnp.bfloat16),
            pltpu.VMEM((8, OWN, 64), jnp.bfloat16),
            pltpu.VMEM((2 * HALF, 64), jnp.float32),
            pltpu.VMEM((2, 16, HALF, 128), jnp.bfloat16),
            dma, dma,
            dma((16,)), dma((16,)),
            dma((8,)), dma((8,)),
            dma((8,)), dma((8,)),
            dma((16,)), dma((16,)),
            dma((16,)), dma((16,)),
        ],
        compiler_params=pltpu.CompilerParams(collective_id=0, has_side_effects=True),
        name="exchange",
    )(packed, params, first, second)


def on_device(
    hidden_in,
    w_query,
    query_gain,
    down_projection_matrix,
    up_projection_matrix,
    query_cotangent,
    first_moment,
    second_moment,
):
    model_width = hidden_in.shape[1]
    rank = down_projection_matrix.shape[1]
    row_count_total = model_width + up_projection_matrix.shape[1]
    own_rows = first_moment.shape[0]
    grad_pre, backward_reduced, scaled_reduced = queries_backward(
        hidden_in,
        query_cotangent,
        w_query,
        query_gain,
        down_projection_matrix,
        up_projection_matrix,
    )
    over_tokens = (((0,), (0,)), ((), ()))
    down_term = lax.dot_general(
        hidden_in, backward_reduced, over_tokens, preferred_element_type=jnp.float32)
    up_term = lax.dot_general(
        grad_pre, scaled_reduced, over_tokens, preferred_element_type=jnp.float32)
    term = jnp.concatenate([down_term, up_term], axis=0)
    packed = term.reshape(NX, 2, NY, 2, HALF, rank).transpose(1, 0, 2, 4, 3, 5)
    packed = packed.reshape(2, NX * NY, HALF, 2 * rank)
    owner = lax.axis_index(("group", "replica"))
    combined = jnp.concatenate([down_projection_matrix, up_projection_matrix.T], axis=0)
    params_own = lax.dynamic_slice_in_dim(combined, owner * own_rows, own_rows, 0).astype(
        jnp.float32
    )
    first_new, second_new, gathered = exchange(packed, params_own, first_moment, second_moment)
    gathered = gathered.reshape(2, NX, NY, HALF, 2, rank).transpose(1, 0, 2, 4, 3, 5)
    gathered = gathered.reshape(row_count_total, rank)
    return (gathered[:model_width], gathered[model_width:].T, first_new, second_new)


def solution(mesh):
    placed = (
        P(("group", "replica"), None),
        P(),
        P(),
        P(),
        P(),
        P(("group", "replica"), None),
        P(("group", "replica"), None),
        P(("group", "replica"), None),
    )
    return jax.shard_map(
        on_device,
        mesh=mesh,
        in_specs=placed,
        out_specs=(P(), P(), P(("group", "replica"), None), P(("group", "replica"), None)),
        check_vma=False,
    )
```

```python
import jax
import jax.numpy as jnp
from jax import lax
from jax.experimental import pallas as pl
from jax.experimental.pallas import tpu as pltpu
from jax.sharding import PartitionSpec as P

adapter_scale_factor = 0.5
norm_epsilon = 1e-06
beta_one = 0.9
beta_two = 0.999
first_bias = 1.0 - 0.9**10
second_bias = 1.0 - 0.999**10
learn_rate = 0.001
adam_eps = 1e-08

MESH = pl.DeviceIdType.MESH
NX, NY, NZH = 4, 4, 4
OWN = 18
HALF = 72
N_DEV = 256
TOK, D, QW, R, HD = 320, 3072, 1536, 64, 128
ROWS = D + QW
WC = 256
NW = QW // WC
XROWS = ROWS // NX
RB = 64

F32, BF16 = jnp.float32, jnp.bfloat16


def adam_update(grads, params, first, second):
    first_new = beta_one * first + (1.0 - beta_one) * grads
    second_new = beta_two * second + (1.0 - beta_two) * grads * grads
    direction = first_new / first_bias / (jnp.sqrt(second_new / second_bias) + adam_eps)
    return ((params - learn_rate * direction).astype(jnp.bfloat16), first_new, second_new)


def hops(d):
    return min(d // 4, 4 - d // 4) + min(d % 4, 4 - d % 4)


def contract(a, b, da, db):
    return lax.dot_general(a, b, (((da,), (db,)), ((), ())), preferred_element_type=F32)


def step_kernel(
    hid_hbm, w_hbm, gain_hbm, dnt_hbm, up_hbm, cot_hbm, m_hbm, v_hbm,
    first_ref, second_ref, g_ref,
    stacked, wbuf, gain, dnt, up, cot, m_ref, v_ref,
    proj, slow, slowt, blt, gt, grows,
    psend, cbuf, qf, qb, xbuf, zsend, zbuf, ubuf, abuf, rows, gbuf,
    ls, ws, cs, cr, xs, xr, zs, zr, us, ur, bs, br, fs, fr,
):
    g = lax.axis_index("group")
    r = lax.axis_index("replica")
    x, zl = g // 2, g % 2
    y, zh, c = r // 8, (r // 2) % 4, r % 2
    t_me = x * NY + y

    def dev(x_, y_, zh_, zl_, c_):
        return (x_ * 2 + zl_, y_ * 8 + zh_ * 2 + c_)

    def rdma(src, dst, ssem, rsem, to):
        return pltpu.make_async_remote_copy(
            src_ref=src, dst_ref=dst, send_sem=ssem, recv_sem=rsem,
            device_id=to, device_id_type=MESH)

    partner = dev(x, y, zh, zl, 1 - c)

    loads = [
        pltpu.make_async_copy(src, dst, ls.at[i])
        for i, (src, dst) in enumerate([
            (hid_hbm, stacked.at[:, :D]), (dnt_hbm, dnt), (up_hbm, up), (cot_hbm, cot),
            (gain_hbm, gain), (m_hbm, m_ref), (v_hbm, v_ref)])
    ]
    wloads = [
        pltpu.make_async_copy(w_hbm.at[:, WC * k : WC * (k + 1)], wbuf.at[k], ws.at[k])
        for k in range(NW)
    ]
    loads[0].start()
    loads[1].start()
    wloads[0].start()
    loads[2].start()
    loads[4].start()
    wloads[1].start()
    loads[3].start()
    for k in range(2, NW):
        wloads[k].start()
    loads[5].start()
    loads[6].start()

    barrier = pltpu.get_barrier_semaphore()
    for d in range(1, 16):
        pl.semaphore_signal(
            barrier, inc=1, device_id_type=MESH,
            device_id=dev((x + d // 4) % NX, (y + d % 4) % NY, zh, zl, c))
    for d in range(1, 16):
        k = (zh * 4 + zl * 2 + c + d) % 16
        pl.semaphore_signal(
            barrier, inc=1, device_id_type=MESH,
            device_id=dev(x, y, k // 4, (k // 2) % 2, k % 2))

    loads[0].wait()
    loads[1].wait()
    low = contract(stacked[:, :D], dnt[...], 1, 1).astype(BF16).astype(F32) * adapter_scale_factor
    slow[...] = low.astype(BF16)
    slowt[...] = low.T.astype(BF16)
    loads[2].wait()
    loads[4].wait()

    def to_rows(j):
        grows[HD * j : HD * (j + 1), :] = gt[:, HD * j : HD * (j + 1)].T

    def backward(k):
        if k == 0:
            loads[3].wait()
        for h in range(2):
            lanes = slice(WC * k + HD * h, WC * k + HD * (h + 1))
            for b in range(TOK // RB):
                tok = slice(RB * b, RB * (b + 1))
                p = proj[k % 2, tok, HD * h : HD * (h + 1)]
                inverse = lax.rsqrt(jnp.mean(p * p, axis=-1, keepdims=True) + norm_epsilon)
                normed = p * inverse
                upstream = cot[tok, lanes].astype(F32) * gain[...]
                along = jnp.mean(upstream * normed, axis=-1, keepdims=True)
                stacked[tok, D + lanes.start : D + lanes.stop] = (
                    inverse * (upstream - normed * along)).astype(BF16)
        lanes = slice(D + WC * k, D + WC * (k + 1))
        gp = stacked[:, lanes]
        back = contract(up[:, WC * k : WC * (k + 1)], gp, 1, 1)
        if k == 0:
            blt[...] = back
        else:
            blt[...] += back
        gt[:, lanes] = jnp.dot(slowt[...], gp, preferred_element_type=F32)
        for j in range(lanes.start // HD, lanes.stop // HD):
            to_rows(j)

    for k in range(NW):
        wloads[k].wait()
        proj[k % 2] = jnp.dot(stacked[:, :D], wbuf[k], preferred_element_type=F32) + jnp.dot(
            slow[...], up[:, WC * k : WC * (k + 1)], preferred_element_type=F32)
        if k:
            backward(k - 1)
    backward(NW - 1)
    back = (adapter_scale_factor * blt[...]).astype(BF16)
    for j in range(D // WC):
        lanes = slice(WC * j, WC * (j + 1))
        gt[:, lanes] = jnp.dot(back, stacked[:, lanes], preferred_element_type=F32)
        to_rows(2 * j)
        to_rows(2 * j + 1)

    def block(x_, zl_, y_):
        o = pl.multiple_of(x_ * XROWS + zl_ * (XROWS // 2) + y_ * 2 * HALF, 8)
        return jnp.concatenate([grows[pl.ds(o, HALF), :], grows[pl.ds(o + HALF, HALF), :]], axis=1)

    pl.semaphore_wait(barrier, 30)

    dxs = (2, 1, 3, 0)
    pair = []
    for i, dx in enumerate(dxs):
        tx = (x + dx) % NX
        for ty in range(NY):
            psend[i, ty] = block(tx, 1 - c, ty)
        cp = rdma(psend.at[i], cbuf.at[i], cs.at[i], cr.at[i], partner)
        cp.start()
        pair.append(cp)

    sends = []
    for i, dx in enumerate(dxs):
        tx = (x + dx) % NX
        pair[i].wait_recv()
        for ty in range(NY):
            qb[i, ty] = (block(tx, c, ty) + cbuf[i, ty]).astype(BF16)
        if dx == 0:
            qf[...] = block(tx, c, y) + cbuf[i, y]
        for dy in (2, 1, 3, 0):
            d = dx * 4 + dy
            if d:
                ty = (y + dy) % NY
                cp = rdma(qb.at[i, ty], xbuf.at[d], xs.at[d], xr.at[d], dev(tx, ty, zh, zl, c))
                cp.start()
                sends.append((d, cp))

    for i in (5, 6):
        loads[i].wait()
    mine = (g * 32 + r) * OWN + lax.broadcasted_iota(jnp.int32, (OWN, D), 0)
    at = lax.broadcasted_iota(jnp.int32, (OWN, D), 1)
    pick_down = (at == mine).astype(F32).astype(BF16)
    pick_up = (at[:, :QW] + D == mine[:, :QW]).astype(F32).astype(BF16)
    params = contract(pick_down, dnt[...], 1, 1) + contract(pick_up, up[...], 1, 1)

    total = qf[...]
    for d, cp in sends:
        cp.wait_recv()
        total = total + xbuf[d].astype(F32)
    for k in range(4):
        zsend[k] = total[OWN * k : OWN * (k + 1)]
    for d, cp in sends:
        cp.wait_send()
    for cp in pair:
        cp.wait_send()

    own_z = zl == c
    zcopies = []
    for dh in range(4):
        for c2 in range(2):
            th = (zh + dh) % NZH
            slab = (th % 2) * 2 + c2
            slot = dh * 2 + zl
            j = dh * 2 + c2
            cp = rdma(zsend.at[slab], zbuf.at[slot], zs.at[j], zr.at[slot], dev(x, y, th, c, c2))
            if dh == 0:
                here = own_z & (c == c2)

                @pl.when(here)
                def _():
                    zbuf[slot] = zsend[slab]

                @pl.when(jnp.logical_not(here))
                def _():
                    cp.start()
            else:
                here = None
                cp.start()
            zcopies.append((cp, here))
    for slot in range(8):
        cp = rdma(zsend.at[0], zbuf.at[slot], zs.at[0], zr.at[slot], partner)
        if slot < 2:
            @pl.when(jnp.logical_not(own_z & (zl == slot)))
            def _():
                cp.wait_recv()
        else:
            cp.wait_recv()
    acc = zbuf[0]
    for slot in range(1, 8):
        acc = acc + zbuf[slot]
    for cp, here in zcopies:
        if here is None:
            cp.wait_send()
        else:
            @pl.when(jnp.logical_not(here))
            def _():
                cp.wait_send()
    grad = jnp.where(zh >= 2, acc[:, 64:], acc[:, :64]) / N_DEV

    updated, first_new, second_new = adam_update(grad, params, m_ref[...], v_ref[...])
    first_ref[...] = first_new
    second_ref[...] = second_new
    ubuf[...] = updated

    k_me = zh * 2 + c
    ucopies = []
    for dh in range(4):
        for l2 in range(2):
            th = (zh + dh) % NZH
            j = dh * 2 + l2
            cp = rdma(ubuf, abuf.at[k_me], us.at[j], ur.at[k_me], dev(x, y, th, l2, zl))
            if dh == 0:
                here = own_z & (zl == l2)

                @pl.when(here)
                def _():
                    abuf[k_me] = ubuf[...]

                @pl.when(jnp.logical_not(here))
                def _():
                    cp.start()
            else:
                here = None
                cp.start()
            ucopies.append((cp, here))
    for k in range(8):
        cp = rdma(ubuf, abuf.at[k], us.at[0], ur.at[k], partner)

        @pl.when(jnp.logical_not(own_z & (k_me == k)))
        def _():
            cp.wait_recv()

        rows[OWN * k : OWN * (k + 1), :] = abuf[k].astype(jnp.float32)
    for cp, here in ucopies:
        if here is None:
            cp.wait_send()
        else:
            @pl.when(jnp.logical_not(here))
            def _():
                cp.wait_send()
    gbuf[c, t_me] = jnp.concatenate([rows[:HALF], rows[HALF:]], axis=1).astype(jnp.bfloat16)

    sends = []
    order = sorted(range(1, 16), key=hops)
    for d in order[::-1]:
        tx, ty = (x + d // 4) % NX, (y + d % 4) % NY
        cp = rdma(gbuf.at[c, t_me], gbuf.at[c, t_me], bs.at[d], br.at[d], dev(tx, ty, zh, zl, c))
        cp.start()
        sends.append(cp)
    forwards = []
    cp = rdma(gbuf.at[c, t_me], gbuf.at[c, t_me], fs.at[0], fr.at[0], partner)
    cp.start()
    forwards.append(cp)
    for d in order:
        src = ((x + NX - d // 4) % NX) * NY + (y + NY - d % 4) % NY
        arrived = rdma(gbuf.at[c, src], gbuf.at[c, src], bs.at[d], br.at[d], partner)
        arrived.wait_recv()
        cp = rdma(gbuf.at[c, src], gbuf.at[c, src], fs.at[d], fr.at[d], partner)
        cp.start()
        forwards.append(cp)
    for cp in sends:
        cp.wait_send()
    for cp in forwards:
        cp.wait_send()
    for d in range(16):
        src = ((x + NX - d // 4) % NX) * NY + (y + NY - d % 4) % NY
        rdma(gbuf.at[1 - c, src], gbuf.at[1 - c, src], fs.at[d], fr.at[d], partner).wait_recv()
    g_ref[...] = gbuf[...]


def unpack_kernel(g_ref, first_in, second_in, down_ref, up_ref, first_ref, second_ref, full):
    for x in range(NX):
        for zl in range(2):
            for y in range(NY):
                o = (x * 8 + zl * 4 + y) * 2 * HALF
                blk = g_ref[zl, x * NY + y].astype(F32)
                full[o : o + HALF, :] = blk[:, :R]
                full[o + HALF : o + 2 * HALF, :] = blk[:, R:]
    for j in range(ROWS // HD):
        tile = full[HD * j : HD * (j + 1), :].T.astype(BF16)
        if j < D // HD:
            down_ref[:, HD * j : HD * (j + 1)] = tile
        else:
            up_ref[:, HD * j - D : HD * (j + 1) - D] = tile
    first_ref[...] = first_in[...]
    second_ref[...] = second_in[...]


def on_device(
    hidden_in,
    w_query,
    query_gain,
    down_projection_matrix,
    up_projection_matrix,
    query_cotangent,
    first_moment,
    second_moment,
):
    vm = pl.BlockSpec(memory_space=pltpu.VMEM)
    anywhere = pl.BlockSpec(memory_space=pl.ANY)
    dma = pltpu.SemaphoreType.DMA
    own = jax.ShapeDtypeStruct((OWN, R), F32)
    first, second, gathered = pl.pallas_call(
        step_kernel,
        out_shape=(own, own, jax.ShapeDtypeStruct((2, 16, HALF, 128), BF16)),
        in_specs=[anywhere] * 8,
        out_specs=(vm,) * 3,
        scratch_shapes=[
            pltpu.VMEM((TOK, ROWS), BF16),
            pltpu.VMEM((NW, D, WC), BF16),
            pltpu.VMEM((1, HD), F32),
            pltpu.VMEM((R, D), BF16),
            pltpu.VMEM((R, QW), BF16),
            pltpu.VMEM((TOK, QW), BF16),
            pltpu.VMEM((OWN, R), F32),
            pltpu.VMEM((OWN, R), F32),
            pltpu.VMEM((2, TOK, WC), F32),
            pltpu.VMEM((TOK, R), BF16),
            pltpu.VMEM((R, TOK), BF16),
            pltpu.VMEM((R, TOK), F32),
            pltpu.VMEM((R, ROWS), F32),
            pltpu.VMEM((ROWS, R), F32),
            pltpu.VMEM((4, 4, HALF, 128), F32),
            pltpu.VMEM((4, 4, HALF, 128), F32),
            pltpu.VMEM((HALF, 128), F32),
            pltpu.VMEM((4, 4, HALF, 128), BF16),
            pltpu.VMEM((16, HALF, 128), BF16),
            pltpu.VMEM((4, OWN, 128), F32),
            pltpu.VMEM((8, OWN, 128), F32),
            pltpu.VMEM((OWN, R), BF16),
            pltpu.VMEM((8, OWN, R), BF16),
            pltpu.VMEM((2 * HALF, R), F32),
            pltpu.VMEM((2, 16, HALF, 128), BF16),
            dma((7,)), dma((NW,)),
            dma((4,)), dma((4,)),
            dma((16,)), dma((16,)),
            dma((8,)), dma((8,)),
            dma((8,)), dma((8,)),
            dma((16,)), dma((16,)),
            dma((16,)), dma((16,)),
        ],
        compiler_params=pltpu.CompilerParams(collective_id=0, has_side_effects=True),
        name="step",
    )(
        hidden_in, w_query, query_gain.reshape(1, HD), down_projection_matrix.T,
        up_projection_matrix, query_cotangent, first_moment, second_moment)
    down, up, first, second = pl.pallas_call(
        unpack_kernel,
        out_shape=(
            jax.ShapeDtypeStruct((R, D), BF16), jax.ShapeDtypeStruct((R, QW), BF16), own, own),
        in_specs=[vm] * 3,
        out_specs=(vm,) * 4,
        scratch_shapes=[pltpu.VMEM((ROWS, R), F32)],
        name="unpack",
    )(gathered, first, second)
    return (down.T, up, first, second)


def solution(mesh):
    placed = (
        P(("group", "replica"), None),
        P(),
        P(),
        P(),
        P(),
        P(("group", "replica"), None),
        P(("group", "replica"), None),
        P(("group", "replica"), None),
    )
    return jax.shard_map(
        on_device,
        mesh=mesh,
        in_specs=placed,
        out_specs=(P(), P(), P(("group", "replica"), None), P(("group", "replica"), None)),
        check_vma=False,
    )
```
